32 devices in a mesh: groups: 2 (over y), pcol: 8 (over z, x), prow: 2 (over core).
Axes of the slice: x: 2, y: 2, z: 4, core: 2. Of those that a mesh axis runs over, the one named last changes fastest.
Arguments:
- leaf_inverse: bfloat16 [512, 128, 128], P(('groups', 'pcol', 'prow')), parts along dimension 0, as said below
- leaf_rhs: bfloat16 [65536, 256], P(('groups', 'pcol', 'prow')), parts along dimension 0, may hold values from -6 to 6
- leaf_coupling: bfloat16 [128, 65536], P(None, ('groups', 'pcol', 'prow')), parts along dimension 1, may hold values from -0.125 to 0.125
- parent: int32 [512], P(('groups', 'pcol', 'prow')), parts along dimension 0, may hold values from 0 to 1
- sep_inverse: float32 [16, 128, 128], P(('groups', 'pcol')), parts along dimension 0, as said below
- sep_coupling: float32 [16, 128, 128], P(('groups', 'pcol')), parts along dimension 0, may hold values from -0.375 to 0.375
- sep_rhs: float32 [2048, 256], P(('groups', 'pcol'), 'prow'), parts along dimension 0, may hold values from -6 to 6
Outputs:
- leaf_solution: bfloat16 [65536, 256], P(('groups', 'pcol', 'prow')), parts along dimension 0
- sep_solution: float32 [2048, 256], P(('groups', 'pcol'), 'prow'), parts along dimension 0
The draws below stay inside these ranges and needn't reach their ends.
There are 2 independent parts, one for each index of `groups`. The reference program is written for one: setup_inputs(seed, part) draws one part's arguments, and reference() takes and returns one part's arrays. A program takes and returns all parts, laid end to end along the dimension named above; each array names one. Nothing has to cross between parts.
Inputs may be any that keep to these rules, and one draw needn't show every extreme that they name: `leaf_inverse`: each block is lower triangular with a positive diagonal. `sep_inverse`: each block is lower triangular with a positive diagonal.
All inputs are finite; a program needn't handle non-finite values.
Results may differ from the reference program's by a relative error of at most 0.0026.
Values sent between devices are 32-bit elements; how exact they have to be, the bound alone decides.
No kernel may reach another device: no remote copies, remote signals or barrier semaphores. Data moves between devices by JAX's collectives and lax.ppermute only.
A program may use at most 128 MiB of HBM per device.

```python
import math
import jax
import jax.numpy as jnp
from jax import lax

BS = 128
RHS = 256
LEAF_DEV = 16
LEAVES = 256
SEPS = 8
N_PCOL = 8
N_PROW = 2


def triangle(key, count):
    key_low, key_diag = jax.random.split(key)
    shape = (count, BS, BS)
    lower = jax.random.normal(key_low, shape, jnp.float32) * math.sqrt(2.0 / BS)
    diag = jnp.exp(jax.random.uniform(key_diag, shape, jnp.float32, -0.35, 0.35))
    rows = lax.broadcasted_iota(jnp.int32, shape, 1)
    cols = lax.broadcasted_iota(jnp.int32, shape, 2)
    return jnp.where(rows > cols, lower, jnp.where(rows == cols, diag, 0.0))


def draw_leaf_inverse(key, part):
    return triangle(jax.random.fold_in(key, 11), LEAVES).astype(jnp.bfloat16)


def draw_sep_inverse(key, part):
    return triangle(jax.random.fold_in(key, 23), SEPS).astype(jnp.float32)


def with_ends(result, own_key, least, top_value):
    longest = result.shape.index(max(result.shape))
    spots = []
    for shift in (0, 1):
        where = [jax.random.randint(jax.random.fold_in(own_key, axis), (), 0, length) for axis, length in enumerate(result.shape)]
        where[longest] = (where[longest] + shift) % result.shape[longest]
        spots.append(tuple(where))
    return result.at[spots[0]].set(least).at[spots[1]].set(top_value)


def levels(own_key, extent, shards, least, top_value):
    level, own = 1.0, jax.random.fold_in(own_key, 6)
    for axis_at, shards_of in shards:
        heights = jnp.exp(jax.random.uniform(jax.random.fold_in(own, axis_at), (shards_of,), jnp.float32, least / len(shards), top_value / len(shards)))
        level = level * jnp.repeat(heights, extent[axis_at] // shards_of).reshape([-1 if axis == axis_at else 1 for axis in range(len(extent))])
    return level


def scatter_about(key, shape, deviation, reach, shards=(), dtype=jnp.bfloat16):
    values = deviation * jax.random.normal(key, shape, jnp.float32)
    if shards:
        values = values * levels(key, shape, shards, -0.22, 0.18)
    return jnp.clip(values, -reach, reach).astype(dtype)


def setup_inputs(seed: int = 0, part: int = 0) -> dict:
    key_list = jax.random.split(jax.random.key(seed), 8)
    own_keys = jax.random.split(jax.random.fold_in(key_list[7], part), 8)
    return {
        "leaf_inverse": draw_leaf_inverse(jax.random.fold_in(jax.random.fold_in(key_list[7], part), 71), part),
        "leaf_rhs": scatter_about(own_keys[1], (LEAVES * BS, RHS), 1.0, 6.0, ((0, 16),)),
        "leaf_coupling": scatter_about(own_keys[2], (BS, LEAVES * BS), (LEAF_DEV * BS) ** -0.5, 0.125, ((1, 16),)),
        "parent": with_ends(jax.random.randint(own_keys[3], (LEAVES,), 0, 2), jax.random.fold_in(own_keys[3], 1), 0, 1).astype(jnp.int32),
        "sep_inverse": draw_sep_inverse(jax.random.fold_in(jax.random.fold_in(key_list[7], part), 71), part),
        "sep_coupling": scatter_about(own_keys[5], (SEPS, BS, BS), (2 * BS) ** -0.5, 0.375, ((0, 8),), jnp.float32),
        "sep_rhs": scatter_about(own_keys[6], (SEPS * BS, RHS), 1.0, 6.0, ((0, 8), (1, 2)), jnp.float32),
    }


def reference(leaf_inverse, leaf_rhs, leaf_coupling, parent, sep_inverse, sep_coupling, sep_rhs):
    blocks = leaf_rhs.astype(jnp.float32).reshape(LEAVES, BS, RHS)
    solved = jnp.einsum('jab,jbr->jar', leaf_inverse.astype(jnp.float32), blocks).astype(jnp.bfloat16)
    group = LEAF_DEV * N_PROW
    coupling_g = leaf_coupling.reshape(BS, N_PCOL, group * BS).transpose(1, 0, 2)
    solved_g = solved.reshape(N_PCOL, group * BS, RHS)
    parent_g = parent.reshape(N_PCOL, group)

    def column_part(items):
        coupling, values, links = items
        own_mask = jnp.repeat((links == 0).astype(jnp.bfloat16), BS)[:, None]
        next_mask = jnp.repeat((links == 1).astype(jnp.bfloat16), BS)[:, None]
        own_sum = jnp.dot(coupling, values * own_mask, preferred_element_type=jnp.float32)
        next_sum = jnp.dot(coupling, values * next_mask, preferred_element_type=jnp.float32)
        return own_sum, next_sum

    own_all, next_all = lax.map(column_part, (coupling_g, solved_g, parent_g))
    arrived = jnp.concatenate([jnp.zeros((1, BS, RHS), jnp.float32), next_all[:-1]], axis=0)
    update = own_all + arrived
    rhs_blocks = sep_rhs.reshape(N_PCOL, BS, RHS)
    hp = lax.Precision.HIGHEST

    def advance(previous, items):
        inverse, coupling, right, upd, first = items
        carried = jnp.dot(coupling, previous, precision=hp) * (1.0 - first)
        current = jnp.dot(inverse, right - upd - carried, precision=hp)
        return current, current

    firsts = (jnp.arange(N_PCOL) == 0).astype(jnp.float32)
    start = jnp.zeros((BS, RHS), jnp.float32)
    unused, solutions = lax.scan(advance, start, (sep_inverse, sep_coupling, rhs_blocks, update, firsts))
    return solved.reshape(LEAVES * BS, RHS), solutions.reshape(N_PCOL * BS, RHS)
```

```python
import jax
import jax.numpy as jnp
from jax import lax
from jax.sharding import PartitionSpec as P


def mul(a, b):
    return jnp.dot(a, b, precision=lax.Precision.HIGH)


def on_device(leaf_inverse, leaf_rhs, leaf_coupling, parent, sep_inverse, sep_coupling, sep_rhs):
    count, block = leaf_inverse.shape[:2]
    width = leaf_rhs.shape[1]
    half = width // 2
    columns = lax.axis_size("pcol")
    column = lax.axis_index("pcol")
    inverse = sep_inverse[0]
    ahead = lax.ppermute(sep_coupling[0], "pcol", [(i, (i - 1) % columns) for i in range(columns)])

    solved = jnp.einsum(
        "jab,jbr->jar",
        leaf_inverse,
        leaf_rhs.reshape(count, block, width),
        preferred_element_type=jnp.float32,
    ).astype(jnp.bfloat16)
    solved = solved.reshape(count * block, width)
    link = jnp.repeat(parent, block)[None, :]
    zero = jnp.zeros_like(leaf_coupling)
    both = jnp.concatenate(
        [jnp.where(link == 0, leaf_coupling, zero), jnp.where(link == 1, leaf_coupling, zero)], 0
    )
    sums = jnp.dot(both, solved, preferred_element_type=jnp.float32)
    row = lax.axis_index("prow")
    left, right = sums[:, :half], sums[:, half:]
    kept = jnp.where(row == 0, left, right)
    sent = jnp.where(row == 0, right, left)
    sums = kept + lax.ppermute(sent, "prow", [(0, 1), (1, 0)])
    own, onward = sums[:block], sums[block:]

    found = mul(inverse, sep_rhs - own)
    weight = inverse
    total = mul(ahead, jnp.concatenate([found, -inverse], 1))
    total = jnp.concatenate([total[:, :half] + onward, total[:, half:]], 1)
    distance = 1
    while distance < columns:
        last = 2 * distance >= columns
        pairs = [(i, i ^ distance) for i in range(columns) if i ^ distance < columns]
        came = lax.ppermute(total[:, :half] if last else total, "pcol", pairs)
        upper = (column & distance) != 0
        came_e = came[:, :half]
        found = jnp.where(upper, found - mul(weight, came_e), found)
        if not last:
            came_b = came[:, half:]
            weight = jnp.where(upper, mul(weight, came_b), weight)
            later = jnp.where(upper, total[:, half:], came_b)
            earlier = jnp.where(upper, came, total)
            add = jnp.where(upper, total[:, :half], came_e)
            made = mul(later, earlier)
            total = jnp.concatenate([made[:, :half] + add, made[:, half:]], 1)
        distance *= 2
    return solved, found


def solution(mesh):
    return jax.shard_map(
        on_device,
        mesh=mesh,
        in_specs=(
            P(("groups", "pcol", "prow"), None, None),
            P(("groups", "pcol", "prow"), None),
            P(None, ("groups", "pcol", "prow")),
            P(("groups", "pcol", "prow")),
            P(("groups", "pcol"), None, None),
            P(("groups", "pcol"), None, None),
            P(("groups", "pcol"), "prow"),
        ),
        out_specs=(P(("groups", "pcol", "prow"), None), P(("groups", "pcol"), "prow")),
        check_vma=False,
    )
```

```python
import jax
import jax.numpy as jnp
from jax import lax
from jax.experimental import pallas as pl
from jax.experimental.pallas import tpu as pltpu
from jax.sharding import PartitionSpec as P

VMEM = pl.BlockSpec(memory_space=pltpu.VMEM)
ANY = pl.BlockSpec(memory_space=pl.ANY)
CHUNKS = 4


def mul(a, b):
    return jnp.dot(a, b, precision=lax.Precision.HIGH)


def leaf_kernel(
    parent_in, inverse_in, rhs_in, coupling_in, right_in, sep_in,
    solved_out, kept, sent, sep_out,
    parent, inverse, rhs, coupling, right, solved, both, sems,
):
    link = pltpu.make_async_copy(parent_in, parent, sems.at[CHUNKS, 3])
    link.start()
    count, block, _ = inverse.shape
    half = kept.shape[1]
    step = count // CHUNKS
    copies = []
    for c in range(CHUNKS):
        leaves = pl.ds(c * step, step)
        rows = pl.ds(c * step * block, step * block)
        copies.append(
            (
                pltpu.make_async_copy(inverse_in.at[leaves], inverse.at[leaves], sems.at[c, 0]),
                pltpu.make_async_copy(rhs_in.at[rows], rhs.at[rows], sems.at[c, 1]),
            )
        )
        for copy in copies[-1]:
            copy.start()
    rest = [
        pltpu.make_async_copy(coupling_in, coupling, sems.at[CHUNKS, 0]),
        pltpu.make_async_copy(right_in, right, sems.at[CHUNKS, 1]),
        pltpu.make_async_copy(sep_in, sep_out, sems.at[CHUNKS, 2]),
    ]
    for copy in rest:
        copy.start()
    outs = []
    for c in range(CHUNKS):
        for copy in copies[c]:
            copy.wait()
        for j in range(c * step, (c + 1) * step):
            rows = pl.ds(j * block, block)
            solved[rows, :] = jnp.dot(
                inverse[j], rhs[rows, :], preferred_element_type=jnp.float32
            ).astype(jnp.bfloat16)
        rows = pl.ds(c * step * block, step * block)
        outs.append(pltpu.make_async_copy(solved.at[rows], solved_out.at[rows], sems.at[c, 2]))
        outs[-1].start()
    link.wait()
    rest[0].wait()
    for j in range(count):
        columns = pl.ds(j * block, block)
        piece = coupling[:, columns]
        zero = jnp.zeros_like(piece)
        both[pl.ds(0, block), columns] = jnp.where(parent[j] == 0, piece, zero)
        both[pl.ds(block, block), columns] = jnp.where(parent[j] == 1, piece, zero)
    sums = jnp.dot(both[...], solved[...], preferred_element_type=jnp.float32)
    first = lax.axis_index("prow") == 0
    sent[...] = jnp.where(first, sums[:, half:], sums[:, :half])
    mine = jnp.where(first, sums[:, :half], sums[:, half:])
    rest[1].wait()
    kept[pl.ds(0, block), :] = mine[:block] - right[...]
    kept[pl.ds(block, block), :] = mine[block:]
    rest[2].wait()
    for out in outs:
        out.wait()


def leaves(parent, inverse, rhs, coupling, right, sep):
    count, block, _ = inverse.shape
    width = rhs.shape[1]
    share = pltpu.VMEM((2 * block, width // 2), jnp.float32)
    return pl.pallas_call(
        leaf_kernel,
        out_shape=(jax.ShapeDtypeStruct(rhs.shape, jnp.bfloat16), share, share, pltpu.VMEM(sep.shape, sep.dtype)),
        in_specs=[ANY] * 6,
        out_specs=(ANY, VMEM, VMEM, VMEM),
        scratch_shapes=[
            pltpu.SMEM(parent.shape, parent.dtype),
            pltpu.VMEM(inverse.shape, inverse.dtype),
            pltpu.VMEM(rhs.shape, rhs.dtype),
            pltpu.VMEM(coupling.shape, coupling.dtype),
            pltpu.VMEM(right.shape, right.dtype),
            pltpu.VMEM(rhs.shape, jnp.bfloat16),
            pltpu.VMEM((2 * block, count * block), jnp.bfloat16),
            pltpu.SemaphoreType.DMA((CHUNKS + 1, 4)),
        ],
        compiler_params=pltpu.CompilerParams(vmem_limit_bytes=16 * 2**20),
    )(*[pltpu.with_memory_space_constraint(a, pltpu.HBM) for a in (parent, inverse, rhs, coupling, right, sep)])


def on_device(leaf_inverse, leaf_rhs, leaf_coupling, parent, sep_inverse, sep_coupling, sep_rhs):
    block = leaf_inverse.shape[1]
    half = leaf_rhs.shape[1] // 2
    columns = lax.axis_size("pcol")
    column = lax.axis_index("pcol")
    ahead = lax.ppermute(sep_coupling[0], "pcol", [(i, i - 1) for i in range(1, columns)])
    solved, kept, sent, inverse = leaves(
        parent, leaf_inverse, leaf_rhs, leaf_coupling, sep_rhs, sep_inverse[0]
    )
    b = -mul(ahead, inverse)
    came = lax.ppermute(sent, "prow", [(0, 1), (1, 0)])
    b, kept = lax.optimization_barrier((b, kept))
    sums = kept + came
    minus, onward = sums[:block], sums[block:]
    weight = inverse
    found = -mul(inverse, minus)
    total = jnp.concatenate([mul(b, minus) + onward, b], 1)
    distance = 1
    while distance < columns:
        last = 2 * distance >= columns
        pairs = [(i, i ^ distance) for i in range(columns) if i ^ distance < columns]
        came = lax.ppermute(total[:, :half] if last else total, "pcol", pairs)
        upper = (column & distance) != 0
        came_e = came[:, :half]
        found = jnp.where(upper, found - mul(weight, came_e), found)
        if not last:
            came_b = came[:, half:]
            weight = jnp.where(upper, mul(weight, came_b), weight)
            later = jnp.where(upper, total[:, half:], came_b)
            earlier = jnp.where(upper, came, total)
            add = jnp.where(upper, total[:, :half], came_e)
            made = mul(later, earlier)
            total = jnp.concatenate([made[:, :half] + add, made[:, half:]], 1)
        distance *= 2
    return solved, found
def solution(mesh):
    return jax.shard_map(
        on_device,
        mesh=mesh,
        in_specs=(
            P(("groups", "pcol", "prow"), None, None),
            P(("groups", "pcol", "prow"), None),
            P(None, ("groups", "pcol", "prow")),
            P(("groups", "pcol", "prow")),
            P(("groups", "pcol"), None, None),
            P(("groups", "pcol"), None, None),
            P(("groups", "pcol"), "prow"),
        ),
        out_specs=(P(("groups", "pcol", "prow"), None), P(("groups", "pcol"), "prow")),
        check_vma=False,
    )
```

```python
import functools

import jax
import jax.numpy as jnp
from jax import lax
from jax.experimental import pallas as pl
from jax.experimental.pallas import tpu as pltpu
from jax.sharding import PartitionSpec as P

VMEM = pl.BlockSpec(memory_space=pltpu.VMEM)
ANY = pl.BlockSpec(memory_space=pl.ANY)
CHUNKS = 2


def mul(a, b):
    return jnp.dot(a, b, precision=lax.Precision.HIGH)


def leaf_kernel(
    parent_in, inverse_in, rhs_in, coupling_in, right_in, sep_in,
    solved, kept, sent, sep_out,
    parent, inverse, rhs, coupling, right, both, sems,
):
    count, block, _ = inverse.shape
    half = kept.shape[1]
    step = count // CHUNKS
    first_copies = [
        pltpu.make_async_copy(parent_in, parent, sems.at[CHUNKS, 0]),
        pltpu.make_async_copy(coupling_in, coupling, sems.at[CHUNKS, 1]),
    ]
    chunk_copies = []
    for c in range(CHUNKS):
        leaves = pl.ds(c * step, step)
        rows = pl.ds(c * step * block, step * block)
        chunk_copies.append(
            [
                pltpu.make_async_copy(inverse_in.at[leaves], inverse.at[leaves], sems.at[c, 0]),
                pltpu.make_async_copy(rhs_in.at[rows], rhs.at[rows], sems.at[c, 1]),
            ]
        )
    last_copies = [
        pltpu.make_async_copy(right_in, right, sems.at[CHUNKS, 2]),
        pltpu.make_async_copy(sep_in, sep_out, sems.at[CHUNKS, 3]),
    ]
    for copy in first_copies + sum(chunk_copies, []) + last_copies:
        copy.start()
    for copy in first_copies:
        copy.wait()
    for j in range(count):
        columns = pl.ds(j * block, block)
        piece = coupling[:, columns]
        zero = jnp.zeros_like(piece)
        both[pl.ds(0, block), columns] = jnp.where(parent[j] == 0, piece, zero)
        both[pl.ds(block, block), columns] = jnp.where(parent[j] == 1, piece, zero)
    sums = None
    for c in range(CHUNKS):
        for copy in chunk_copies[c]:
            copy.wait()
        for j in range(c * step, (c + 1) * step):
            rows = pl.ds(j * block, block)
            solved[rows, :] = jnp.dot(
                inverse[j], rhs[rows, :], preferred_element_type=jnp.float32
            ).astype(jnp.bfloat16)
        rows = pl.ds(c * step * block, step * block)
        part = jnp.dot(both[:, rows], solved[rows, :], preferred_element_type=jnp.float32)
        sums = part if c == 0 else sums + part
    first = lax.axis_index("prow") == 0
    sent[...] = jnp.where(first, sums[:, half:], sums[:, :half])
    mine = jnp.where(first, sums[:, :half], sums[:, half:])
    for copy in last_copies:
        copy.wait()
    kept[pl.ds(0, block), :] = mine[:block] - right[...]
    kept[pl.ds(block, block), :] = mine[block:]


def leaves(parent, inverse, rhs, coupling, right, sep):
    count, block, _ = inverse.shape
    width = rhs.shape[1]
    share = pltpu.VMEM((2 * block, width // 2), jnp.float32)
    return pl.pallas_call(
        leaf_kernel,
        out_shape=(pltpu.VMEM(rhs.shape, jnp.bfloat16), share, share, pltpu.VMEM(sep.shape, sep.dtype)),
        in_specs=[ANY] * 6,
        out_specs=(VMEM, VMEM, VMEM, VMEM),
        scratch_shapes=[
            pltpu.SMEM(parent.shape, parent.dtype),
            pltpu.VMEM(inverse.shape, inverse.dtype),
            pltpu.VMEM(rhs.shape, rhs.dtype),
            pltpu.VMEM(coupling.shape, coupling.dtype),
            pltpu.VMEM(right.shape, right.dtype),
            pltpu.VMEM((2 * block, count * block), jnp.bfloat16),
            pltpu.SemaphoreType.DMA((CHUNKS + 1, 4)),
        ],
        compiler_params=pltpu.CompilerParams(vmem_limit_bytes=16 * 2**20),
    )(*[pltpu.with_memory_space_constraint(a, pltpu.HBM) for a in (parent, inverse, rhs, coupling, right, sep)])


def store_kernel(solved, after, out, sem):
    copy = pltpu.make_async_copy(solved, out, sem)
    copy.start()
    copy.wait()


def store(array, after):
    return pl.pallas_call(
        store_kernel,
        out_shape=pltpu.HBM(array.shape, array.dtype),
        in_specs=[VMEM, ANY],
        out_specs=ANY,
        scratch_shapes=[pltpu.SemaphoreType.DMA],
        cost_estimate=pl.CostEstimate(flops=0, bytes_accessed=2**16, transcendentals=0),
    )(*[pltpu.with_memory_space_constraint(a, pltpu.VMEM) for a in (array, after)])


def split(a):
    high = a.astype(jnp.bfloat16)
    return high, (a - high.astype(jnp.float32)).astype(jnp.bfloat16)


def product(a, b):
    def dot(x, y):
        return jnp.dot(x, y, preferred_element_type=jnp.float32)

    (ah, al), (bh, bl) = split(a), split(b)
    return dot(ah, bh) + (dot(ah, bl) + dot(al, bh))


def finish_kernel(distance, found, weight, came, written, out, result, sem):
    del written

    @pl.when((lax.axis_index("pcol") & distance) != 0)
    def _():
        result[...] = found[...] - product(weight[...], came[...])
        copy = pltpu.make_async_copy(result, out, sem)
        copy.start()
        copy.wait()


def finish(distance, found, weight, came):
    written = store(found, weight)
    return pl.pallas_call(
        functools.partial(finish_kernel, distance),
        out_shape=pltpu.HBM(found.shape, found.dtype),
        in_specs=[VMEM, VMEM, VMEM, ANY],
        out_specs=ANY,
        scratch_shapes=[pltpu.VMEM(found.shape, found.dtype), pltpu.SemaphoreType.DMA],
        input_output_aliases={3: 0},
        cost_estimate=pl.CostEstimate(flops=0, bytes_accessed=2**16, transcendentals=0),
    )(*[pltpu.with_memory_space_constraint(a, pltpu.VMEM) for a in (found, weight, came)], written)


def on_device(leaf_inverse, leaf_rhs, leaf_coupling, parent, sep_inverse, sep_coupling, sep_rhs):
    block = leaf_inverse.shape[1]
    half = leaf_rhs.shape[1] // 2
    columns = lax.axis_size("pcol")
    column = lax.axis_index("pcol")
    ahead = lax.ppermute(sep_coupling[0], "pcol", [(i, i - 1) for i in range(1, columns)])
    solved, kept, sent, inverse = leaves(
        parent, leaf_inverse, leaf_rhs, leaf_coupling, sep_rhs, sep_inverse[0]
    )
    b = -mul(ahead, inverse)
    came = lax.ppermute(sent, "prow", [(0, 1), (1, 0)])
    b, kept = lax.optimization_barrier((b, kept))
    sums = kept + came
    minus, onward = sums[:block], sums[block:]
    weight = inverse
    found = -mul(inverse, minus)
    total = jnp.concatenate([mul(b, minus) + onward, b], 1)
    def join(lower, higher):
        made = mul(higher[:, half:], lower)
        return jnp.concatenate([made[:, :half] + higher[:, :half], made[:, half:]], 1)

    def swap(array, distance):
        pairs = [(i, i ^ distance) for i in range(columns) if i ^ distance < columns]
        return lax.ppermute(array, "pcol", pairs)

    late = []
    distance = 1
    flights = {d: swap(total, d) for d in (1, 2, 3)}
    while distance < columns:
        last = 2 * distance >= columns
        if distance == 1:
            came = flights[1]
        elif distance == 2:
            odd = (column & 1) != 0
            came = join(
                jnp.where(odd, flights[3], flights[2]), jnp.where(odd, flights[2], flights[3])
            )
        else:
            total = total[:, :half] if last else total
            came = swap(total, distance)
        if last:
            late, total_after = lax.optimization_barrier((late, total))
            for above, block_came in late:
                moved = mul(weight, block_came)
                found = jnp.where(above, found - moved[:, :half], found)
                weight = jnp.where(above, moved[:, half:], weight)
            solved = store(solved, total_after)
            found = finish(distance, found, weight, came)
            break
        upper = (column & distance) != 0
        late.append((upper, came))
        total = join(jnp.where(upper, came, total), jnp.where(upper, total, came))
        distance *= 2
    return solved, found
def solution(mesh):
    return jax.shard_map(
        on_device,
        mesh=mesh,
        in_specs=(
            P(("groups", "pcol", "prow"), None, None),
            P(("groups", "pcol", "prow"), None),
            P(None, ("groups", "pcol", "prow")),
            P(("groups", "pcol", "prow")),
            P(("groups", "pcol"), None, None),
            P(("groups", "pcol"), None, None),
            P(("groups", "pcol"), "prow"),
        ),
        out_specs=(P(("groups", "pcol", "prow"), None), P(("groups", "pcol"), "prow")),
        check_vma=False,
    )
```

```python
import functools

import jax
import jax.numpy as jnp
from jax import lax
from jax.experimental import pallas as pl
from jax.experimental.pallas import tpu as pltpu
from jax.sharding import PartitionSpec as P

VMEM = pl.BlockSpec(memory_space=pltpu.VMEM)
ANY = pl.BlockSpec(memory_space=pl.ANY)
CHUNKS = 2


def mul(a, b):
    return jnp.dot(a, b, precision=lax.Precision.HIGH)


def leaf_kernel(
    parent_in, inverse_in, rhs_in, coupling_in, right_in, sep_in,
    solved, kept, sent, sep_out,
    parent, inverse, rhs, coupling, right, both, sems,
):
    count, block, _ = inverse.shape
    half = kept.shape[1]
    step = count // CHUNKS
    first_copies = [
        pltpu.make_async_copy(parent_in, parent, sems.at[CHUNKS, 0]),
        pltpu.make_async_copy(coupling_in, coupling, sems.at[CHUNKS, 1]),
    ]
    chunk_copies = []
    for c in range(CHUNKS):
        leaves = pl.ds(c * step, step)
        rows = pl.ds(c * step * block, step * block)
        chunk_copies.append(
            [
                pltpu.make_async_copy(inverse_in.at[leaves], inverse.at[leaves], sems.at[c, 0]),
                pltpu.make_async_copy(rhs_in.at[rows], rhs.at[rows], sems.at[c, 1]),
            ]
        )
    last_copies = [
        pltpu.make_async_copy(right_in, right, sems.at[CHUNKS, 2]),
        pltpu.make_async_copy(sep_in, sep_out, sems.at[CHUNKS, 3]),
    ]
    for copy in first_copies + sum(chunk_copies, []) + last_copies:
        copy.start()
    for copy in first_copies:
        copy.wait()
    for j in range(count):
        columns = pl.ds(j * block, block)
        piece = coupling[:, columns]
        zero = jnp.zeros_like(piece)
        both[pl.ds(0, block), columns] = jnp.where(parent[j] == 0, piece, zero)
        both[pl.ds(block, block), columns] = jnp.where(parent[j] == 1, piece, zero)
    sums = None
    for c in range(CHUNKS):
        for copy in chunk_copies[c]:
            copy.wait()
        for j in range(c * step, (c + 1) * step):
            rows = pl.ds(j * block, block)
            solved[rows, :] = jnp.dot(
                inverse[j], rhs[rows, :], preferred_element_type=jnp.float32
            ).astype(jnp.bfloat16)
        rows = pl.ds(c * step * block, step * block)
        part = jnp.dot(both[:, rows], solved[rows, :], preferred_element_type=jnp.float32)
        sums = part if c == 0 else sums + part
    first = lax.axis_index("prow") == 0
    sent[...] = jnp.where(first, sums[:, half:], sums[:, :half])
    mine = jnp.where(first, sums[:, :half], sums[:, half:])
    for copy in last_copies:
        copy.wait()
    kept[pl.ds(0, block), :] = mine[:block] - right[...]
    kept[pl.ds(block, block), :] = mine[block:]


def leaves(parent, inverse, rhs, coupling, right, sep):
    count, block, _ = inverse.shape
    width = rhs.shape[1]
    share = pltpu.VMEM((2 * block, width // 2), jnp.float32)
    return pl.pallas_call(
        leaf_kernel,
        out_shape=(pltpu.VMEM(rhs.shape, jnp.bfloat16), share, share, pltpu.VMEM(sep.shape, sep.dtype)),
        in_specs=[ANY] * 6,
        out_specs=(VMEM, VMEM, VMEM, VMEM),
        scratch_shapes=[
            pltpu.SMEM(parent.shape, parent.dtype),
            pltpu.VMEM(inverse.shape, inverse.dtype),
            pltpu.VMEM(rhs.shape, rhs.dtype),
            pltpu.VMEM(coupling.shape, coupling.dtype),
            pltpu.VMEM(right.shape, right.dtype),
            pltpu.VMEM((2 * block, count * block), jnp.bfloat16),
            pltpu.SemaphoreType.DMA((CHUNKS + 1, 4)),
        ],
        compiler_params=pltpu.CompilerParams(vmem_limit_bytes=16 * 2**20),
    )(*[pltpu.with_memory_space_constraint(a, pltpu.HBM) for a in (parent, inverse, rhs, coupling, right, sep)])


def store_kernel(solved, after, out, sem):
    copy = pltpu.make_async_copy(solved, out, sem)
    copy.start()
    copy.wait()


def store(array, after):
    return pl.pallas_call(
        store_kernel,
        out_shape=pltpu.HBM(array.shape, array.dtype),
        in_specs=[VMEM, ANY],
        out_specs=ANY,
        scratch_shapes=[pltpu.SemaphoreType.DMA],
        cost_estimate=pl.CostEstimate(flops=0, bytes_accessed=2**16, transcendentals=0),
    )(*[pltpu.with_memory_space_constraint(a, pltpu.VMEM) for a in (array, after)])


def split(a):
    high = a.astype(jnp.bfloat16)
    return high, (a - high.astype(jnp.float32)).astype(jnp.bfloat16)


def product(a, b):
    def dot(x, y):
        return jnp.dot(x, y, preferred_element_type=jnp.float32)

    (ah, al), (bh, bl) = split(a), split(b)
    return dot(ah, bh) + (dot(ah, bl) + dot(al, bh))


def finish_kernel(distance, found, weight, came, written, out, result, sem):
    del written

    @pl.when((lax.axis_index("pcol") & distance) != 0)
    def _():
        result[...] = found[...] - product(weight[...], came[...])
        copy = pltpu.make_async_copy(result, out, sem)
        copy.start()
        copy.wait()


def finish(distance, found, weight, came):
    written = store(found, weight)
    return pl.pallas_call(
        functools.partial(finish_kernel, distance),
        out_shape=pltpu.HBM(found.shape, found.dtype),
        in_specs=[VMEM, VMEM, VMEM, ANY],
        out_specs=ANY,
        scratch_shapes=[pltpu.VMEM(found.shape, found.dtype), pltpu.SemaphoreType.DMA],
        input_output_aliases={3: 0},
        cost_estimate=pl.CostEstimate(flops=0, bytes_accessed=2**16, transcendentals=0),
    )(*[pltpu.with_memory_space_constraint(a, pltpu.VMEM) for a in (found, weight, came)], written)


def on_device(leaf_inverse, leaf_rhs, leaf_coupling, parent, sep_inverse, sep_coupling, sep_rhs):
    block = leaf_inverse.shape[1]
    half = leaf_rhs.shape[1] // 2
    columns = lax.axis_size("pcol")
    column = lax.axis_index("pcol")
    own = sep_coupling[0]
    n = columns
    ring = [(2, 1), (1, 0), (0, 2), (n - 2, n - 3), (n - 3, n - 1), (n - 1, n - 2)]
    ring += [(2 * k - a, 2 * k - 1 + a) for k in range(2, n // 2 - 1) for a in (0, 1)]
    def odd_from():
        return lax.ppermute(own, "pcol", ring)
    def even_from():
        return lax.ppermute(own, "pcol", [(i, i ^ 1) for i in range(n)])
    o = odd_from()
    e = even_from()
    ahead = jnp.where((column & 1) == 0, e, o)
    solved, kept, sent, inverse = leaves(
        parent, leaf_inverse, leaf_rhs, leaf_coupling, sep_rhs, sep_inverse[0]
    )
    b = -mul(ahead, inverse)
    came = lax.ppermute(sent, "prow", [(0, 1), (1, 0)])
    b, kept = lax.optimization_barrier((b, kept))
    sums = kept + came
    minus, onward = sums[:block], sums[block:]
    weight = inverse
    found = -mul(inverse, minus)
    total = jnp.concatenate([mul(b, minus) + onward, b], 1)
    def join(lower, higher):
        made = mul(higher[:, half:], lower)
        return jnp.concatenate([made[:, :half] + higher[:, :half], made[:, half:]], 1)

    def swap(array, distance):
        pairs = [(i, i ^ distance) for i in range(columns) if i ^ distance < columns]
        return lax.ppermute(array, "pcol", pairs)

    late = []
    distance = 1
    flights = dict(zip((3, 2, 1), lax.optimization_barrier([swap(total, d) for d in (3, 2, 1)])))
    while distance < columns:
        last = 2 * distance >= columns
        if distance == 1:
            came = flights[1]
        elif distance == 2:
            odd = (column & 1) != 0
            came = join(
                jnp.where(odd, flights[3], flights[2]), jnp.where(odd, flights[2], flights[3])
            )
        else:
            total = total[:, :half] if last else total
            came = swap(total, distance)
        if last:
            late, total_after = lax.optimization_barrier((late, total))
            for above, block_came in late:
                moved = mul(weight, block_came)
                found = jnp.where(above, found - moved[:, :half], found)
                weight = jnp.where(above, moved[:, half:], weight)
            solved = store(solved, total_after)
            found = finish(distance, found, weight, came)
            break
        upper = (column & distance) != 0
        late.append((upper, came))
        total = join(jnp.where(upper, came, total), jnp.where(upper, total, came))
        distance *= 2
    return solved, found
def solution(mesh):
    return jax.shard_map(
        on_device,
        mesh=mesh,
        in_specs=(
            P(("groups", "pcol", "prow"), None, None),
            P(("groups", "pcol", "prow"), None),
            P(None, ("groups", "pcol", "prow")),
            P(("groups", "pcol", "prow")),
            P(("groups", "pcol"), None, None),
            P(("groups", "pcol"), None, None),
            P(("groups", "pcol"), "prow"),
        ),
        out_specs=(P(("groups", "pcol", "prow"), None), P(("groups", "pcol"), "prow")),
        check_vma=False,
    )
```

```python
import functools

import jax
import jax.numpy as jnp
from jax import lax
from jax.experimental import pallas as pl
from jax.experimental.pallas import tpu as pltpu
from jax.sharding import PartitionSpec as P

VMEM = pl.BlockSpec(memory_space=pltpu.VMEM)
ANY = pl.BlockSpec(memory_space=pl.ANY)
CHUNKS = 2


def mul(a, b):
    return jnp.dot(a, b, precision=lax.Precision.HIGH)


def leaf_kernel(
    parent_in, inverse_in, rhs_in, coupling_in, right_in, sep_in,
    solved, kept, sent, sep_out,
    parent, inverse, rhs, coupling, right, both, sems,
):
    count, block, _ = inverse.shape
    half = kept.shape[1]
    step = count // CHUNKS
    first_copies = [
        pltpu.make_async_copy(parent_in, parent, sems.at[CHUNKS, 0]),
        pltpu.make_async_copy(coupling_in, coupling, sems.at[CHUNKS, 1]),
    ]
    chunk_copies = []
    for c in range(CHUNKS):
        leaves = pl.ds(c * step, step)
        rows = pl.ds(c * step * block, step * block)
        chunk_copies.append(
            [
                pltpu.make_async_copy(inverse_in.at[leaves], inverse.at[leaves], sems.at[c, 0]),
                pltpu.make_async_copy(rhs_in.at[rows], rhs.at[rows], sems.at[c, 1]),
            ]
        )
    last_copies = [
        pltpu.make_async_copy(right_in, right, sems.at[CHUNKS, 2]),
        pltpu.make_async_copy(sep_in, sep_out, sems.at[CHUNKS, 3]),
    ]
    for copy in first_copies + sum(chunk_copies, []) + last_copies:
        copy.start()
    for copy in first_copies:
        copy.wait()
    for j in range(count):
        columns = pl.ds(j * block, block)
        piece = coupling[:, columns]
        zero = jnp.zeros_like(piece)
        both[pl.ds(0, block), columns] = jnp.where(parent[j] == 0, piece, zero)
        both[pl.ds(block, block), columns] = jnp.where(parent[j] == 1, piece, zero)
    sums = None
    for c in range(CHUNKS):
        for copy in chunk_copies[c]:
            copy.wait()
        for j in range(c * step, (c + 1) * step):
            rows = pl.ds(j * block, block)
            solved[rows, :] = jnp.dot(
                inverse[j], rhs[rows, :], preferred_element_type=jnp.float32
            ).astype(jnp.bfloat16)
        rows = pl.ds(c * step * block, step * block)
        part = jnp.dot(both[:, rows], solved[rows, :], preferred_element_type=jnp.float32)
        sums = part if c == 0 else sums + part
    first = lax.axis_index("prow") == 0
    sent[...] = jnp.where(first, sums[:, half:], sums[:, :half])
    mine = jnp.where(first, sums[:, :half], sums[:, half:])
    for copy in last_copies:
        copy.wait()
    kept[pl.ds(0, block), :] = mine[:block] - right[...]
    kept[pl.ds(block, block), :] = mine[block:]


def leaves(parent, inverse, rhs, coupling, right, sep):
    count, block, _ = inverse.shape
    width = rhs.shape[1]
    share = pltpu.VMEM((2 * block, width // 2), jnp.float32)
    return pl.pallas_call(
        leaf_kernel,
        out_shape=(pltpu.VMEM(rhs.shape, jnp.bfloat16), share, share, pltpu.VMEM(sep.shape, sep.dtype)),
        in_specs=[ANY] * 6,
        out_specs=(VMEM, VMEM, VMEM, VMEM),
        scratch_shapes=[
            pltpu.SMEM(parent.shape, parent.dtype),
            pltpu.VMEM(inverse.shape, inverse.dtype),
            pltpu.VMEM(rhs.shape, rhs.dtype),
            pltpu.VMEM(coupling.shape, coupling.dtype),
            pltpu.VMEM(right.shape, right.dtype),
            pltpu.VMEM((2 * block, count * block), jnp.bfloat16),
            pltpu.SemaphoreType.DMA((CHUNKS + 1, 4)),
        ],
        compiler_params=pltpu.CompilerParams(vmem_limit_bytes=16 * 2**20),
    )(*[pltpu.with_memory_space_constraint(a, pltpu.HBM) for a in (parent, inverse, rhs, coupling, right, sep)])


def store_kernel(solved, after, out, sem):
    copy = pltpu.make_async_copy(solved, out, sem)
    copy.start()
    copy.wait()


def store(array, after):
    return pl.pallas_call(
        store_kernel,
        out_shape=pltpu.HBM(array.shape, array.dtype),
        in_specs=[VMEM, ANY],
        out_specs=ANY,
        scratch_shapes=[pltpu.SemaphoreType.DMA],
        cost_estimate=pl.CostEstimate(flops=0, bytes_accessed=2**16, transcendentals=0),
    )(*[pltpu.with_memory_space_constraint(a, pltpu.VMEM) for a in (array, after)])


def split(a):
    high = a.astype(jnp.bfloat16)
    return high, (a - high.astype(jnp.float32)).astype(jnp.bfloat16)


def product(a, b):
    def dot(x, y):
        return jnp.dot(x, y, preferred_element_type=jnp.float32)

    (ah, al), (bh, bl) = split(a), split(b)
    return dot(ah, bh) + (dot(ah, bl) + dot(al, bh))


def top_kernel(own, near, across, far, out):
    column = lax.axis_index("pcol")
    odd = (column & 1) != 0
    high = (column & 2) != 0
    half = out.shape[1]
    low_own, high_own = jnp.where(odd, near[...], own[...]), jnp.where(odd, own[...], near[...])
    low_other = jnp.where(odd, far[...], across[...])
    high_other = jnp.where(odd, across[...], far[...])
    first = jnp.where(high, low_other, low_own)
    second = jnp.where(high, high_other, high_own)
    third = jnp.where(high, low_own, low_other)
    fourth = jnp.where(high, high_own, high_other)
    lower = second[:, :half] + product(second[:, half:], first[:, :half])
    upper = product(fourth[:, half:], third)
    out[...] = fourth[:, :half] + upper[:, :half] + product(upper[:, half:], lower)


def top(own, near, across, far):
    block, width = own.shape
    return pl.pallas_call(
        top_kernel,
        out_shape=pltpu.VMEM((block, width // 2), own.dtype),
        in_specs=[VMEM] * 4,
        out_specs=VMEM,
        cost_estimate=pl.CostEstimate(flops=0, bytes_accessed=2**16, transcendentals=0),
    )(*[pltpu.with_memory_space_constraint(a, pltpu.VMEM) for a in (own, near, across, far)])


def finish_kernel(distance, found, weight, came, written, out, result, sem):
    del written

    @pl.when((lax.axis_index("pcol") & distance) != 0)
    def _():
        result[...] = found[...] - product(weight[...], came[...])
        copy = pltpu.make_async_copy(result, out, sem)
        copy.start()
        copy.wait()


def finish(distance, found, weight, came):
    written = store(found, weight)
    return pl.pallas_call(
        functools.partial(finish_kernel, distance),
        out_shape=pltpu.HBM(found.shape, found.dtype),
        in_specs=[VMEM, VMEM, VMEM, ANY],
        out_specs=ANY,
        scratch_shapes=[pltpu.VMEM(found.shape, found.dtype), pltpu.SemaphoreType.DMA],
        input_output_aliases={3: 0},
        cost_estimate=pl.CostEstimate(flops=0, bytes_accessed=2**16, transcendentals=0),
    )(*[pltpu.with_memory_space_constraint(a, pltpu.VMEM) for a in (found, weight, came)], written)


def on_device(leaf_inverse, leaf_rhs, leaf_coupling, parent, sep_inverse, sep_coupling, sep_rhs):
    block = leaf_inverse.shape[1]
    half = leaf_rhs.shape[1] // 2
    columns = lax.axis_size("pcol")
    column = lax.axis_index("pcol")
    own = sep_coupling[0]
    n = columns
    ring = [(2, 1), (1, 0), (0, 2), (n - 2, n - 3), (n - 3, n - 1), (n - 1, n - 2)]
    ring += [(2 * k - a, 2 * k - 1 + a) for k in range(2, n // 2 - 1) for a in (0, 1)]
    def odd_from():
        return lax.ppermute(own, "pcol", ring)
    def even_from():
        return lax.ppermute(own, "pcol", [(i, i ^ 1) for i in range(n)])
    o = odd_from()
    e = even_from()
    ahead = jnp.where((column & 1) == 0, e, o)
    solved, kept, sent, inverse = leaves(
        parent, leaf_inverse, leaf_rhs, leaf_coupling, sep_rhs, sep_inverse[0]
    )
    b = -mul(ahead, inverse)
    came = lax.ppermute(sent, "prow", [(0, 1), (1, 0)])
    b, kept = lax.optimization_barrier((b, kept))
    sums = kept + came
    minus, onward = sums[:block], sums[block:]
    weight = inverse
    found = -mul(inverse, minus)
    total = jnp.concatenate([mul(b, minus) + onward, b], 1)
    def join(lower, higher):
        made = mul(higher[:, half:], lower)
        return jnp.concatenate([made[:, :half] + higher[:, :half], made[:, half:]], 1)

    def swap(array, distance):
        pairs = [(i, i ^ distance) for i in range(columns) if i ^ distance < columns]
        return lax.ppermute(array, "pcol", pairs)

    flights = {}
    order = (2, 1, 3)
    arrived = lax.optimization_barrier([swap(total, d) for d in order])
    flights = dict(zip(order, arrived))
    odd = (column & 1) != 0

    def other_pair(pieces):
        return join(jnp.where(odd, pieces[3], pieces[2]), jnp.where(odd, pieces[2], pieces[3]))

    if columns == 8:
        total = top(total, flights[1], flights[2], flights[3])
        late = ()
    else:
        late = ((1, flights[1]), (2, other_pair(flights)))
        for distance, came in late:
            upper = (column & distance) != 0
            total = join(jnp.where(upper, came, total), jnp.where(upper, total, came))
    distance = 4
    while 2 * distance < columns:
        came = swap(total, distance)
        upper = (column & distance) != 0
        late += ((distance, came),)
        total = join(jnp.where(upper, came, total), jnp.where(upper, total, came))
        distance *= 2
    total = total[:, :half]
    came = swap(total, distance)
    flights, late, total = lax.optimization_barrier((flights, late, total))
    if columns == 8:
        late = ((1, flights[1]), (2, other_pair(flights)))
    for place, block_came in late:
        above = (column & place) != 0
        moved = mul(weight, block_came)
        found = jnp.where(above, found - moved[:, :half], found)
        weight = jnp.where(above, moved[:, half:], weight)
    solved = store(solved, total)
    found = finish(distance, found, weight, came)
    return solved, found
def solution(mesh):
    return jax.shard_map(
        on_device,
        mesh=mesh,
        in_specs=(
            P(("groups", "pcol", "prow"), None, None),
            P(("groups", "pcol", "prow"), None),
            P(None, ("groups", "pcol", "prow")),
            P(("groups", "pcol", "prow")),
            P(("groups", "pcol"), None, None),
            P(("groups", "pcol"), None, None),
            P(("groups", "pcol"), "prow"),
        ),
        out_specs=(P(("groups", "pcol", "prow"), None), P(("groups", "pcol"), "prow")),
        check_vma=False,
    )
```

```python
import functools

import jax
import jax.numpy as jnp
from jax import lax
from jax.experimental import pallas as pl
from jax.experimental.pallas import tpu as pltpu
from jax.sharding import PartitionSpec as P

VMEM = pl.BlockSpec(memory_space=pltpu.VMEM)
ANY = pl.BlockSpec(memory_space=pl.ANY)
CHUNKS = 2


def mul(a, b):
    return jnp.dot(a, b, precision=lax.Precision.HIGH)


def leaf_kernel(
    parent_in, inverse_in, rhs_in, coupling_in, right_in, sep_in,
    solved, kept, sent, sep_out,
    parent, inverse, rhs, coupling, right, both, sems,
):
    count, block, _ = inverse.shape
    half = kept.shape[1]
    step = count // CHUNKS
    first_copies = [
        pltpu.make_async_copy(parent_in, parent, sems.at[CHUNKS, 0]),
        pltpu.make_async_copy(coupling_in, coupling, sems.at[CHUNKS, 1]),
    ]
    chunk_copies = []
    for c in range(CHUNKS):
        leaves = pl.ds(c * step, step)
        rows = pl.ds(c * step * block, step * block)
        chunk_copies.append(
            [
                pltpu.make_async_copy(inverse_in.at[leaves], inverse.at[leaves], sems.at[c, 0]),
                pltpu.make_async_copy(rhs_in.at[rows], rhs.at[rows], sems.at[c, 1]),
            ]
        )
    last_copies = [
        pltpu.make_async_copy(right_in, right, sems.at[CHUNKS, 2]),
        pltpu.make_async_copy(sep_in, sep_out, sems.at[CHUNKS, 3]),
    ]
    for copy in first_copies + sum(chunk_copies, []) + last_copies:
        copy.start()
    for copy in first_copies:
        copy.wait()
    for j in range(count):
        columns = pl.ds(j * block, block)
        piece = coupling[:, columns]
        zero = jnp.zeros_like(piece)
        both[pl.ds(0, block), columns] = jnp.where(parent[j] == 0, piece, zero)
        both[pl.ds(block, block), columns] = jnp.where(parent[j] == 1, piece, zero)
    sums = None
    for c in range(CHUNKS):
        for copy in chunk_copies[c]:
            copy.wait()
        for j in range(c * step, (c + 1) * step):
            rows = pl.ds(j * block, block)
            solved[rows, :] = jnp.dot(
                inverse[j], rhs[rows, :], preferred_element_type=jnp.float32
            ).astype(jnp.bfloat16)
        rows = pl.ds(c * step * block, step * block)
        part = jnp.dot(both[:, rows], solved[rows, :], preferred_element_type=jnp.float32)
        sums = part if c == 0 else sums + part
    first = lax.axis_index("prow") == 0
    sent[...] = jnp.where(first, sums[:, half:], sums[:, :half])
    mine = jnp.where(first, sums[:, :half], sums[:, half:])
    for copy in last_copies:
        copy.wait()
    kept[pl.ds(0, block), :] = mine[:block] - right[...]
    kept[pl.ds(block, block), :] = mine[block:]


def leaves(parent, inverse, rhs, coupling, right, sep):
    count, block, _ = inverse.shape
    width = rhs.shape[1]
    share = pltpu.VMEM((2 * block, width // 2), jnp.float32)
    return pl.pallas_call(
        leaf_kernel,
        out_shape=(pltpu.VMEM(rhs.shape, jnp.bfloat16), share, share, pltpu.VMEM(sep.shape, sep.dtype)),
        in_specs=[ANY] * 6,
        out_specs=(VMEM, VMEM, VMEM, VMEM),
        scratch_shapes=[
            pltpu.SMEM(parent.shape, parent.dtype),
            pltpu.VMEM(inverse.shape, inverse.dtype),
            pltpu.VMEM(rhs.shape, rhs.dtype),
            pltpu.VMEM(coupling.shape, coupling.dtype),
            pltpu.VMEM(right.shape, right.dtype),
            pltpu.VMEM((2 * block, count * block), jnp.bfloat16),
            pltpu.SemaphoreType.DMA((CHUNKS + 1, 4)),
        ],
        compiler_params=pltpu.CompilerParams(vmem_limit_bytes=16 * 2**20),
    )(*[pltpu.with_memory_space_constraint(a, pltpu.HBM) for a in (parent, inverse, rhs, coupling, right, sep)])


def store_kernel(solved, after, out, sem):
    copy = pltpu.make_async_copy(solved, out, sem)
    copy.start()
    copy.wait()


def store(array, after):
    return pl.pallas_call(
        store_kernel,
        out_shape=pltpu.HBM(array.shape, array.dtype),
        in_specs=[VMEM, ANY],
        out_specs=ANY,
        scratch_shapes=[pltpu.SemaphoreType.DMA],
        cost_estimate=pl.CostEstimate(flops=0, bytes_accessed=2**16, transcendentals=0),
    )(*[pltpu.with_memory_space_constraint(a, pltpu.VMEM) for a in (array, after)])


def split(a):
    high = a.astype(jnp.bfloat16)
    return high, (a - high.astype(jnp.float32)).astype(jnp.bfloat16)


def product(a, b):
    def dot(x, y):
        return jnp.dot(x, y, preferred_element_type=jnp.float32)

    (ah, al), (bh, bl) = split(a), split(b)
    return dot(ah, bh) + (dot(ah, bl) + dot(al, bh))


def top_kernel(own, near, across, far, out):
    column = lax.axis_index("pcol")
    odd = (column & 1) != 0
    high = (column & 2) != 0
    half = out.shape[1]
    low_own, high_own = jnp.where(odd, near[...], own[...]), jnp.where(odd, own[...], near[...])
    low_other = jnp.where(odd, far[...], across[...])
    high_other = jnp.where(odd, across[...], far[...])
    first = jnp.where(high, low_other, low_own)
    second = jnp.where(high, high_other, high_own)
    third = jnp.where(high, low_own, low_other)
    fourth = jnp.where(high, high_own, high_other)
    lower = second[:, :half] + product(second[:, half:], first[:, :half])
    upper = product(fourth[:, half:], third)
    out[...] = fourth[:, :half] + upper[:, :half] + product(upper[:, half:], lower)


def top(own, near, across, far):
    block, width = own.shape
    return pl.pallas_call(
        top_kernel,
        out_shape=pltpu.VMEM((block, width // 2), own.dtype),
        in_specs=[VMEM] * 4,
        out_specs=VMEM,
        cost_estimate=pl.CostEstimate(flops=0, bytes_accessed=2**16, transcendentals=0),
    )(*[pltpu.with_memory_space_constraint(a, pltpu.VMEM) for a in (own, near, across, far)])


def finish_kernel(distance, found, weight, came, written, out, result, sem):
    del written

    @pl.when((lax.axis_index("pcol") & distance) != 0)
    def _():
        result[...] = found[...] - product(weight[...], came[...])
        copy = pltpu.make_async_copy(result, out, sem)
        copy.start()
        copy.wait()


def finish(distance, found, weight, came):
    written = store(found, weight)
    return pl.pallas_call(
        functools.partial(finish_kernel, distance),
        out_shape=pltpu.HBM(found.shape, found.dtype),
        in_specs=[VMEM, VMEM, VMEM, ANY],
        out_specs=ANY,
        scratch_shapes=[pltpu.VMEM(found.shape, found.dtype), pltpu.SemaphoreType.DMA],
        input_output_aliases={3: 0},
        cost_estimate=pl.CostEstimate(flops=0, bytes_accessed=2**16, transcendentals=0),
    )(*[pltpu.with_memory_space_constraint(a, pltpu.VMEM) for a in (found, weight, came)], written)


def on_device(leaf_inverse, leaf_rhs, leaf_coupling, parent, sep_inverse, sep_coupling, sep_rhs):
    block = leaf_inverse.shape[1]
    half = leaf_rhs.shape[1] // 2
    columns = lax.axis_size("pcol")
    column = lax.axis_index("pcol")
    n = columns
    row = lax.axis_index("prow")
    ring = [(2, 1), (1, 0), (0, 2), (n - 2, n - 3), (n - 3, n - 1), (n - 1, n - 2)]
    ring += [(2 * k - a, 2 * k - 1 + a) for k in range(2, n // 2 - 1) for a in (0, 1)]
    shift = [(2 * i, 2 * (i ^ 1)) for i in range(n)] + [(2 * i + 1, 2 * j + 1) for i, j in ring]
    ahead = lax.ppermute(sep_coupling[0], ("pcol", "prow"), shift)
    solved, kept, sent, inverse = leaves(
        parent, leaf_inverse, leaf_rhs, leaf_coupling, sep_rhs, sep_inverse[0]
    )
    came = lax.ppermute(sent, "prow", [(0, 1), (1, 0)])
    b = -mul(ahead, inverse)
    b, came = lax.optimization_barrier((b, came))
    other_b = lax.ppermute(b, "prow", [(0, 1), (1, 0)])
    b = jnp.where((column & 1) == row, b, other_b)
    sums = kept + came
    minus, onward = sums[:block], sums[block:]
    weight = inverse
    found = -mul(inverse, minus)
    total = jnp.concatenate([mul(b, minus) + onward, b], 1)
    def join(lower, higher):
        made = mul(higher[:, half:], lower)
        return jnp.concatenate([made[:, :half] + higher[:, :half], made[:, half:]], 1)

    def swap(array, distance):
        pairs = [(i, i ^ distance) for i in range(columns) if i ^ distance < columns]
        return lax.ppermute(array, "pcol", pairs)

    flights = {}
    order = (1, 2, 3)
    arrived = lax.optimization_barrier([swap(total, d) for d in order])
    flights = dict(zip(order, arrived))
    odd = (column & 1) != 0

    def other_pair(pieces):
        return join(jnp.where(odd, pieces[3], pieces[2]), jnp.where(odd, pieces[2], pieces[3]))

    if columns == 8:
        total = top(total, flights[1], flights[2], flights[3])
        late = ()
    else:
        late = ((1, flights[1]), (2, other_pair(flights)))
        for distance, came in late:
            upper = (column & distance) != 0
            total = join(jnp.where(upper, came, total), jnp.where(upper, total, came))
    distance = 4
    while 2 * distance < columns:
        came = swap(total, distance)
        upper = (column & distance) != 0
        late += ((distance, came),)
        total = join(jnp.where(upper, came, total), jnp.where(upper, total, came))
        distance *= 2
    total = total[:, :half]
    came = swap(total, distance)
    flights, late, total = lax.optimization_barrier((flights, late, total))
    if columns == 8:
        late = ((1, flights[1]), (2, other_pair(flights)))
    for place, block_came in late:
        above = (column & place) != 0
        moved = mul(weight, block_came)
        found = jnp.where(above, found - moved[:, :half], found)
        weight = jnp.where(above, moved[:, half:], weight)
    solved = store(solved, total)
    found = finish(distance, found, weight, came)
    return solved, found
def solution(mesh):
    return jax.shard_map(
        on_device,
        mesh=mesh,
        in_specs=(
            P(("groups", "pcol", "prow"), None, None),
            P(("groups", "pcol", "prow"), None),
            P(None, ("groups", "pcol", "prow")),
            P(("groups", "pcol", "prow")),
            P(("groups", "pcol"), None, None),
            P(("groups", "pcol"), None, None),
            P(("groups", "pcol"), "prow"),
        ),
        out_specs=(P(("groups", "pcol", "prow"), None), P(("groups", "pcol"), "prow")),
        check_vma=False,
    )
```

```python
import functools

import jax
import jax.numpy as jnp
from jax import lax
from jax.experimental import pallas as pl
from jax.experimental.pallas import tpu as pltpu
from jax.sharding import PartitionSpec as P

VMEM = pl.BlockSpec(memory_space=pltpu.VMEM)
ANY = pl.BlockSpec(memory_space=pl.ANY)
CHUNKS = 2


def mul(a, b):
    return jnp.dot(a, b, precision=lax.Precision.HIGH)


def leaf_kernel(
    parent_in, inverse_in, rhs_in, coupling_in, right_in, sep_in,
    solved, kept, sent, sep_out,
    parent, inverse, rhs, coupling, right, both, sems,
):
    count, block, _ = inverse.shape
    half = kept.shape[1]
    step = count // CHUNKS
    first_copies = [
        pltpu.make_async_copy(parent_in, parent, sems.at[CHUNKS, 0]),
        pltpu.make_async_copy(coupling_in, coupling, sems.at[CHUNKS, 1]),
    ]
    chunk_copies = []
    for c in range(CHUNKS):
        leaves = pl.ds(c * step, step)
        rows = pl.ds(c * step * block, step * block)
        chunk_copies.append(
            [
                pltpu.make_async_copy(inverse_in.at[leaves], inverse.at[leaves], sems.at[c, 0]),
                pltpu.make_async_copy(rhs_in.at[rows], rhs.at[rows], sems.at[c, 1]),
            ]
        )
    last_copies = [
        pltpu.make_async_copy(right_in, right, sems.at[CHUNKS, 2]),
        pltpu.make_async_copy(sep_in, sep_out, sems.at[CHUNKS, 3]),
    ]
    for copy in first_copies + sum(chunk_copies, []) + last_copies:
        copy.start()
    for copy in first_copies:
        copy.wait()
    for j in range(count):
        columns = pl.ds(j * block, block)
        piece = coupling[:, columns]
        zero = jnp.zeros_like(piece)
        both[pl.ds(0, block), columns] = jnp.where(parent[j] == 0, piece, zero)
        both[pl.ds(block, block), columns] = jnp.where(parent[j] == 1, piece, zero)
    sums = None
    for c in range(CHUNKS):
        for copy in chunk_copies[c]:
            copy.wait()
        for j in range(c * step, (c + 1) * step):
            rows = pl.ds(j * block, block)
            solved[rows, :] = jnp.dot(
                inverse[j], rhs[rows, :], preferred_element_type=jnp.float32
            ).astype(jnp.bfloat16)
        rows = pl.ds(c * step * block, step * block)
        part = jnp.dot(both[:, rows], solved[rows, :], preferred_element_type=jnp.float32)
        sums = part if c == 0 else sums + part
    first = lax.axis_index("prow") == 0
    sent[...] = jnp.where(first, sums[:, half:], sums[:, :half])
    mine = jnp.where(first, sums[:, :half], sums[:, half:])
    for copy in last_copies:
        copy.wait()
    kept[pl.ds(0, block), :] = mine[:block] - right[...]
    kept[pl.ds(block, block), :] = mine[block:]


def leaves(parent, inverse, rhs, coupling, right, sep):
    count, block, _ = inverse.shape
    width = rhs.shape[1]
    share = pltpu.VMEM((2 * block, width // 2), jnp.float32)
    return pl.pallas_call(
        leaf_kernel,
        out_shape=(pltpu.VMEM(rhs.shape, jnp.bfloat16), share, share, pltpu.VMEM(sep.shape, sep.dtype)),
        in_specs=[ANY] * 6,
        out_specs=(VMEM, VMEM, VMEM, VMEM),
        scratch_shapes=[
            pltpu.SMEM(parent.shape, parent.dtype),
            pltpu.VMEM(inverse.shape, inverse.dtype),
            pltpu.VMEM(rhs.shape, rhs.dtype),
            pltpu.VMEM(coupling.shape, coupling.dtype),
            pltpu.VMEM(right.shape, right.dtype),
            pltpu.VMEM((2 * block, count * block), jnp.bfloat16),
            pltpu.SemaphoreType.DMA((CHUNKS + 1, 4)),
        ],
        compiler_params=pltpu.CompilerParams(vmem_limit_bytes=16 * 2**20),
    )(*[pltpu.with_memory_space_constraint(a, pltpu.HBM) for a in (parent, inverse, rhs, coupling, right, sep)])


def store_kernel(solved, after, out, sem):
    copy = pltpu.make_async_copy(solved, out, sem)
    copy.start()
    copy.wait()


def store(array, after):
    return pl.pallas_call(
        store_kernel,
        out_shape=pltpu.HBM(array.shape, array.dtype),
        in_specs=[VMEM, ANY],
        out_specs=ANY,
        scratch_shapes=[pltpu.SemaphoreType.DMA],
        cost_estimate=pl.CostEstimate(flops=0, bytes_accessed=2**16, transcendentals=0),
    )(*[pltpu.with_memory_space_constraint(a, pltpu.VMEM) for a in (array, after)])


def split(a):
    high = a.astype(jnp.bfloat16)
    return high, (a - high.astype(jnp.float32)).astype(jnp.bfloat16)


def product(a, b):
    (ah, al), (bh, bl) = split(a), split(b)
    wide = jnp.concatenate([ah, ah, al], 1)
    tall = jnp.concatenate([bh, bl, bh], 0)
    return jnp.dot(wide, tall, preferred_element_type=jnp.float32)


def top_kernel(own, near, across, far, out):
    column = lax.axis_index("pcol")
    odd = (column & 1) != 0
    high = (column & 2) != 0
    half = out.shape[1]
    low_own, high_own = jnp.where(odd, near[...], own[...]), jnp.where(odd, own[...], near[...])
    low_other = jnp.where(odd, far[...], across[...])
    high_other = jnp.where(odd, across[...], far[...])
    first = jnp.where(high, low_other, low_own)
    second = jnp.where(high, high_other, high_own)
    third = jnp.where(high, low_own, low_other)
    fourth = jnp.where(high, high_own, high_other)
    lower = second[:, :half] + product(second[:, half:], first[:, :half])
    upper = product(fourth[:, half:], third)
    out[...] = fourth[:, :half] + upper[:, :half] + product(upper[:, half:], lower)


def top(own, near, across, far):
    block, width = own.shape
    return pl.pallas_call(
        top_kernel,
        out_shape=pltpu.VMEM((block, width // 2), own.dtype),
        in_specs=[VMEM] * 4,
        out_specs=VMEM,
        cost_estimate=pl.CostEstimate(flops=0, bytes_accessed=2**16, transcendentals=0),
    )(*[pltpu.with_memory_space_constraint(a, pltpu.VMEM) for a in (own, near, across, far)])


def finish_kernel(distance, found, weight, came, written, out, result, sem):
    del written

    @pl.when((lax.axis_index("pcol") & distance) != 0)
    def _():
        result[...] = found[...] - product(weight[...], came[...])
        copy = pltpu.make_async_copy(result, out, sem)
        copy.start()
        copy.wait()


def finish(distance, found, weight, came):
    written = store(found, weight)
    return pl.pallas_call(
        functools.partial(finish_kernel, distance),
        out_shape=pltpu.HBM(found.shape, found.dtype),
        in_specs=[VMEM, VMEM, VMEM, ANY],
        out_specs=ANY,
        scratch_shapes=[pltpu.VMEM(found.shape, found.dtype), pltpu.SemaphoreType.DMA],
        input_output_aliases={3: 0},
        cost_estimate=pl.CostEstimate(flops=0, bytes_accessed=2**16, transcendentals=0),
    )(*[pltpu.with_memory_space_constraint(a, pltpu.VMEM) for a in (found, weight, came)], written)


def on_device(leaf_inverse, leaf_rhs, leaf_coupling, parent, sep_inverse, sep_coupling, sep_rhs):
    block = leaf_inverse.shape[1]
    half = leaf_rhs.shape[1] // 2
    columns = lax.axis_size("pcol")
    column = lax.axis_index("pcol")
    n = columns
    row = lax.axis_index("prow")
    ring = [(2, 1), (1, 0), (0, 2), (n - 2, n - 3), (n - 3, n - 1), (n - 1, n - 2)]
    ring += [(2 * k - a, 2 * k - 1 + a) for k in range(2, n // 2 - 1) for a in (0, 1)]
    shift = [(2 * i, 2 * (i ^ 1)) for i in range(n)] + [(2 * i + 1, 2 * j + 1) for i, j in ring]
    ahead = lax.ppermute(sep_coupling[0], ("pcol", "prow"), shift)
    solved, kept, sent, inverse = leaves(
        parent, leaf_inverse, leaf_rhs, leaf_coupling, sep_rhs, sep_inverse[0]
    )
    came = lax.ppermute(sent, "prow", [(0, 1), (1, 0)])
    b = -mul(ahead, inverse)
    b, came = lax.optimization_barrier((b, came))
    other_b = lax.ppermute(b, "prow", [(0, 1), (1, 0)])
    b = jnp.where((column & 1) == row, b, other_b)
    sums = kept + came
    minus, onward = sums[:block], sums[block:]
    weight = inverse
    found = -mul(inverse, minus)
    total = jnp.concatenate([mul(b, minus) + onward, b], 1)
    def join(lower, higher):
        made = mul(higher[:, half:], lower)
        return jnp.concatenate([made[:, :half] + higher[:, :half], made[:, half:]], 1)

    def swap(array, distance):
        pairs = [(i, i ^ distance) for i in range(columns) if i ^ distance < columns]
        return lax.ppermute(array, "pcol", pairs)

    flights = {}
    order = (1, 2, 3)
    arrived = lax.optimization_barrier([swap(total, d) for d in order])
    flights = dict(zip(order, arrived))
    odd = (column & 1) != 0

    def other_pair(pieces):
        return join(jnp.where(odd, pieces[3], pieces[2]), jnp.where(odd, pieces[2], pieces[3]))

    if columns == 8:
        total = top(total, flights[1], flights[2], flights[3])
        late = ()
    else:
        late = ((1, flights[1]), (2, other_pair(flights)))
        for distance, came in late:
            upper = (column & distance) != 0
            total = join(jnp.where(upper, came, total), jnp.where(upper, total, came))
    distance = 4
    while 2 * distance < columns:
        came = swap(total, distance)
        upper = (column & distance) != 0
        late += ((distance, came),)
        total = join(jnp.where(upper, came, total), jnp.where(upper, total, came))
        distance *= 2
    total = total[:, :half]
    came = swap(total, distance)
    flights, late, total = lax.optimization_barrier((flights, late, total))
    if columns == 8:
        late = ((1, flights[1]), (2, other_pair(flights)))
    for place, block_came in late:
        above = (column & place) != 0
        moved = mul(weight, block_came)
        found = jnp.where(above, found - moved[:, :half], found)
        weight = jnp.where(above, moved[:, half:], weight)
    solved = store(solved, total)
    found = finish(distance, found, weight, came)
    return solved, found
def solution(mesh):
    return jax.shard_map(
        on_device,
        mesh=mesh,
        in_specs=(
            P(("groups", "pcol", "prow"), None, None),
            P(("groups", "pcol", "prow"), None),
            P(None, ("groups", "pcol", "prow")),
            P(("groups", "pcol", "prow")),
            P(("groups", "pcol"), None, None),
            P(("groups", "pcol"), None, None),
            P(("groups", "pcol"), "prow"),
        ),
        out_specs=(P(("groups", "pcol", "prow"), None), P(("groups", "pcol"), "prow")),
        check_vma=False,
    )
```

```python
import functools

import jax
import jax.numpy as jnp
from jax import lax
from jax.experimental import pallas as pl
from jax.experimental.pallas import tpu as pltpu
from jax.sharding import PartitionSpec as P

VMEM = pl.BlockSpec(memory_space=pltpu.VMEM)
ANY = pl.BlockSpec(memory_space=pl.ANY)
CHUNKS = 2


def mul(a, b):
    return jnp.dot(a, b, precision=lax.Precision.HIGH)


def leaf_kernel(
    parent_in, inverse_in, rhs_in, coupling_in, right_in, sep_in,
    solved, kept, sent, sep_out,
    parent, inverse, rhs, coupling, right, both, sems,
):
    count, block, _ = inverse.shape
    half = kept.shape[1]
    step = count // CHUNKS
    first_copies = [
        pltpu.make_async_copy(parent_in, parent, sems.at[CHUNKS, 0]),
        pltpu.make_async_copy(coupling_in, coupling, sems.at[CHUNKS, 1]),
    ]
    chunk_copies = []
    for c in range(CHUNKS):
        leaves = pl.ds(c * step, step)
        rows = pl.ds(c * step * block, step * block)
        chunk_copies.append(
            [
                pltpu.make_async_copy(inverse_in.at[leaves], inverse.at[leaves], sems.at[c, 0]),
                pltpu.make_async_copy(rhs_in.at[rows], rhs.at[rows], sems.at[c, 1]),
            ]
        )
    last_copies = [
        pltpu.make_async_copy(right_in, right, sems.at[CHUNKS, 2]),
        pltpu.make_async_copy(sep_in, sep_out, sems.at[CHUNKS, 3]),
    ]
    for copy in first_copies + sum(chunk_copies, []) + last_copies:
        copy.start()
    for copy in first_copies:
        copy.wait()
    for j in range(count):
        columns = pl.ds(j * block, block)
        piece = coupling[:, columns]
        zero = jnp.zeros_like(piece)
        both[pl.ds(0, block), columns] = jnp.where(parent[j] == 0, piece, zero)
        both[pl.ds(block, block), columns] = jnp.where(parent[j] == 1, piece, zero)
    sums = None
    for c in range(CHUNKS):
        for copy in chunk_copies[c]:
            copy.wait()
        for j in range(c * step, (c + 1) * step):
            rows = pl.ds(j * block, block)
            solved[rows, :] = jnp.dot(
                inverse[j], rhs[rows, :], preferred_element_type=jnp.float32
            ).astype(jnp.bfloat16)
        rows = pl.ds(c * step * block, step * block)
        part = jnp.dot(both[:, rows], solved[rows, :], preferred_element_type=jnp.float32)
        sums = part if c == 0 else sums + part
    first = lax.axis_index("prow") == 0
    sent[...] = jnp.where(first, sums[:, half:], sums[:, :half])
    mine = jnp.where(first, sums[:, :half], sums[:, half:])
    for copy in last_copies:
        copy.wait()
    kept[pl.ds(0, block), :] = mine[:block] - right[...]
    kept[pl.ds(block, block), :] = mine[block:]


def leaves(parent, inverse, rhs, coupling, right, sep):
    count, block, _ = inverse.shape
    width = rhs.shape[1]
    share = pltpu.VMEM((2 * block, width // 2), jnp.float32)
    return pl.pallas_call(
        leaf_kernel,
        out_shape=(pltpu.VMEM(rhs.shape, jnp.bfloat16), share, share, pltpu.VMEM(sep.shape, sep.dtype)),
        in_specs=[ANY] * 6,
        out_specs=(VMEM, VMEM, VMEM, VMEM),
        scratch_shapes=[
            pltpu.SMEM(parent.shape, parent.dtype),
            pltpu.VMEM(inverse.shape, inverse.dtype),
            pltpu.VMEM(rhs.shape, rhs.dtype),
            pltpu.VMEM(coupling.shape, coupling.dtype),
            pltpu.VMEM(right.shape, right.dtype),
            pltpu.VMEM((2 * block, count * block), jnp.bfloat16),
            pltpu.SemaphoreType.DMA((CHUNKS + 1, 4)),
        ],
        compiler_params=pltpu.CompilerParams(vmem_limit_bytes=16 * 2**20),
    )(*[pltpu.with_memory_space_constraint(a, pltpu.HBM) for a in (parent, inverse, rhs, coupling, right, sep)])


def store_kernel(solved, after, out, sem):
    copy = pltpu.make_async_copy(solved, out, sem)
    copy.start()
    copy.wait()


def store(array, after):
    return pl.pallas_call(
        store_kernel,
        out_shape=pltpu.HBM(array.shape, array.dtype),
        in_specs=[VMEM, ANY],
        out_specs=ANY,
        scratch_shapes=[pltpu.SemaphoreType.DMA],
        cost_estimate=pl.CostEstimate(flops=0, bytes_accessed=2**16, transcendentals=0),
    )(*[pltpu.with_memory_space_constraint(a, pltpu.VMEM) for a in (array, after)])


def split(a):
    high = a.astype(jnp.bfloat16)
    return high, (a - high.astype(jnp.float32)).astype(jnp.bfloat16)


def product(a, b):
    (ah, al), (bh, bl) = split(a), split(b)
    wide = jnp.concatenate([ah, ah, al], 1)
    tall = jnp.concatenate([bh, bl, bh], 0)
    return jnp.dot(wide, tall, preferred_element_type=jnp.float32)


def top_kernel(own, near, across, far, out):
    column = lax.axis_index("pcol")
    odd = (column & 1) != 0
    high = (column & 2) != 0
    half = out.shape[1]
    low_own, high_own = jnp.where(odd, near[...], own[...]), jnp.where(odd, own[...], near[...])
    low_other = jnp.where(odd, far[...], across[...])
    high_other = jnp.where(odd, across[...], far[...])
    first = jnp.where(high, low_other, low_own)
    second = jnp.where(high, high_other, high_own)
    third = jnp.where(high, low_own, low_other)
    fourth = jnp.where(high, high_own, high_other)
    lower = second[:, :half] + product(second[:, half:], first[:, :half])
    upper = product(fourth[:, half:], third)
    out[...] = fourth[:, :half] + upper[:, :half] + product(upper[:, half:], lower)


def top(own, near, across, far):
    block, width = own.shape
    return pl.pallas_call(
        top_kernel,
        out_shape=pltpu.VMEM((block, width // 2), own.dtype),
        in_specs=[VMEM] * 4,
        out_specs=VMEM,
        cost_estimate=pl.CostEstimate(flops=0, bytes_accessed=2**16, transcendentals=0),
    )(*[pltpu.with_memory_space_constraint(a, pltpu.VMEM) for a in (own, near, across, far)])


def finish_kernel(distance, found, weight, came, written, out, result, sem):
    del written

    @pl.when((lax.axis_index("pcol") & distance) != 0)
    def _():
        result[...] = found[...] - product(weight[...], came[...])
        copy = pltpu.make_async_copy(result, out, sem)
        copy.start()
        copy.wait()


def finish(distance, found, weight, came):
    written = store(found, weight)
    return pl.pallas_call(
        functools.partial(finish_kernel, distance),
        out_shape=pltpu.HBM(found.shape, found.dtype),
        in_specs=[VMEM, VMEM, VMEM, ANY],
        out_specs=ANY,
        scratch_shapes=[pltpu.VMEM(found.shape, found.dtype), pltpu.SemaphoreType.DMA],
        input_output_aliases={3: 0},
        cost_estimate=pl.CostEstimate(flops=0, bytes_accessed=2**16, transcendentals=0),
    )(*[pltpu.with_memory_space_constraint(a, pltpu.VMEM) for a in (found, weight, came)], written)


def on_device(leaf_inverse, leaf_rhs, leaf_coupling, parent, sep_inverse, sep_coupling, sep_rhs):
    block = leaf_inverse.shape[1]
    half = leaf_rhs.shape[1] // 2
    columns = lax.axis_size("pcol")
    column = lax.axis_index("pcol")
    n = columns
    row = lax.axis_index("prow")
    ring = [(2, 1), (1, 0), (0, 2), (n - 2, n - 3), (n - 3, n - 1), (n - 1, n - 2)]
    ring += [(2 * k - a, 2 * k - 1 + a) for k in range(2, n // 2 - 1) for a in (0, 1)]
    shift = [(2 * i, 2 * (i ^ 1)) for i in range(n)] + [(2 * i + 1, 2 * j + 1) for i, j in ring]
    ahead = lax.ppermute(sep_coupling[0], ("pcol", "prow"), shift)
    solved, kept, sent, inverse = leaves(
        parent, leaf_inverse, leaf_rhs, leaf_coupling, sep_rhs, sep_inverse[0]
    )
    came = lax.ppermute(sent, "prow", [(0, 1), (1, 0)])
    b = -mul(ahead, inverse)
    b, came = lax.optimization_barrier((b, came))
    other_b = lax.ppermute(b, "prow", [(0, 1), (1, 0)])
    b = jnp.where((column & 1) == row, b, other_b)
    sums = kept + came
    minus, onward = sums[:block], sums[block:]
    weight = inverse
    found = -mul(inverse, minus)
    total = jnp.concatenate([mul(b, minus) + onward, b], 1)
    def join(lower, higher):
        made = mul(higher[:, half:], lower)
        return jnp.concatenate([made[:, :half] + higher[:, :half], made[:, half:]], 1)

    def swap(array, distance):
        pairs = [(i, i ^ distance) for i in range(columns) if i ^ distance < columns]
        return lax.ppermute(array, "pcol", pairs)

    flights = {}
    def mixed(first, second):
        pairs = [
            (2 * i + r, 2 * (i ^ d) + r)
            for i in range(columns)
            for r, d in ((0, first), (1, second))
            if i ^ d < columns
        ]
        return lax.ppermute(total, ("pcol", "prow"), pairs)

    arrived = lax.optimization_barrier([mixed(*(1, 2)), mixed(*(2, 1)), mixed(*(3, 3))])
    flights = {}
    for d in (1, 2, 3):
        flights[d] = jnp.where(row == 0, arrived[{1: 0, 2: 1, 3: 2}[d]], arrived[{2: 0, 1: 1, 3: 2}[d]])
    odd = (column & 1) != 0

    def other_pair(pieces):
        return join(jnp.where(odd, pieces[3], pieces[2]), jnp.where(odd, pieces[2], pieces[3]))

    if columns == 8:
        total = top(total, flights[1], flights[2], flights[3])
        late = ()
    else:
        late = ((1, flights[1]), (2, other_pair(flights)))
        for distance, came in late:
            upper = (column & distance) != 0
            total = join(jnp.where(upper, came, total), jnp.where(upper, total, came))
    distance = 4
    while 2 * distance < columns:
        came = swap(total, distance)
        upper = (column & distance) != 0
        late += ((distance, came),)
        total = join(jnp.where(upper, came, total), jnp.where(upper, total, came))
        distance *= 2
    total = total[:, :half]
    came = swap(total, distance)
    flights, late, total = lax.optimization_barrier((flights, late, total))
    if columns == 8:
        late = ((1, flights[1]), (2, other_pair(flights)))
    for place, block_came in late:
        above = (column & place) != 0
        moved = mul(weight, block_came)
        found = jnp.where(above, found - moved[:, :half], found)
        weight = jnp.where(above, moved[:, half:], weight)
    solved = store(solved, total)
    found = finish(distance, found, weight, came)
    return solved, found
def solution(mesh):
    return jax.shard_map(
        on_device,
        mesh=mesh,
        in_specs=(
            P(("groups", "pcol", "prow"), None, None),
            P(("groups", "pcol", "prow"), None),
            P(None, ("groups", "pcol", "prow")),
            P(("groups", "pcol", "prow")),
            P(("groups", "pcol"), None, None),
            P(("groups", "pcol"), None, None),
            P(("groups", "pcol"), "prow"),
        ),
        out_specs=(P(("groups", "pcol", "prow"), None), P(("groups", "pcol"), "prow")),
        check_vma=False,
    )
```

```python
import functools

import jax
import jax.numpy as jnp
from jax import lax
from jax.experimental import pallas as pl
from jax.experimental.pallas import tpu as pltpu
from jax.sharding import PartitionSpec as P

VMEM = pl.BlockSpec(memory_space=pltpu.VMEM)
ANY = pl.BlockSpec(memory_space=pl.ANY)
CHUNKS = 2


def mul(a, b):
    return jnp.dot(a, b, precision=lax.Precision.HIGH)


def leaf_kernel(
    parent_in, inverse_in, rhs_in, coupling_in, right_in, sep_in,
    solved, kept, sent, sep_out,
    parent, inverse, rhs, coupling, right, both, sems,
):
    count, block, _ = inverse.shape
    half = kept.shape[1]
    step = count // CHUNKS
    first_copies = [
        pltpu.make_async_copy(parent_in, parent, sems.at[CHUNKS, 0]),
        pltpu.make_async_copy(coupling_in, coupling, sems.at[CHUNKS, 1]),
    ]
    chunk_copies = []
    for c in range(CHUNKS):
        leaves = pl.ds(c * step, step)
        rows = pl.ds(c * step * block, step * block)
        chunk_copies.append(
            [
                pltpu.make_async_copy(inverse_in.at[leaves], inverse.at[leaves], sems.at[c, 0]),
                pltpu.make_async_copy(rhs_in.at[rows], rhs.at[rows], sems.at[c, 1]),
            ]
        )
    last_copies = [
        pltpu.make_async_copy(right_in, right, sems.at[CHUNKS, 2]),
        pltpu.make_async_copy(sep_in, sep_out, sems.at[CHUNKS, 3]),
    ]
    for copy in first_copies + sum(chunk_copies, []) + last_copies:
        copy.start()
    for copy in first_copies:
        copy.wait()
    for j in range(count):
        columns = pl.ds(j * block, block)
        piece = coupling[:, columns]
        zero = jnp.zeros_like(piece)
        both[pl.ds(0, block), columns] = jnp.where(parent[j] == 0, piece, zero)
        both[pl.ds(block, block), columns] = jnp.where(parent[j] == 1, piece, zero)
    sums = None
    for c in range(CHUNKS):
        for copy in chunk_copies[c]:
            copy.wait()
        for j in range(c * step, (c + 1) * step):
            rows = pl.ds(j * block, block)
            solved[rows, :] = jnp.dot(
                inverse[j], rhs[rows, :], preferred_element_type=jnp.float32
            ).astype(jnp.bfloat16)
        rows = pl.ds(c * step * block, step * block)
        part = jnp.dot(both[:, rows], solved[rows, :], preferred_element_type=jnp.float32)
        sums = part if c == 0 else sums + part
    first = lax.axis_index("prow") == 0
    sent[...] = jnp.where(first, sums[:, half:], sums[:, :half])
    mine = jnp.where(first, sums[:, :half], sums[:, half:])
    for copy in last_copies:
        copy.wait()
    kept[pl.ds(0, block), :] = mine[:block] - right[...]
    kept[pl.ds(block, block), :] = mine[block:]


def leaves(parent, inverse, rhs, coupling, right, sep):
    count, block, _ = inverse.shape
    width = rhs.shape[1]
    share = pltpu.VMEM((2 * block, width // 2), jnp.float32)
    return pl.pallas_call(
        leaf_kernel,
        out_shape=(pltpu.VMEM(rhs.shape, jnp.bfloat16), share, share, pltpu.VMEM(sep.shape, sep.dtype)),
        in_specs=[ANY] * 6,
        out_specs=(VMEM, VMEM, VMEM, VMEM),
        scratch_shapes=[
            pltpu.SMEM(parent.shape, parent.dtype),
            pltpu.VMEM(inverse.shape, inverse.dtype),
            pltpu.VMEM(rhs.shape, rhs.dtype),
            pltpu.VMEM(coupling.shape, coupling.dtype),
            pltpu.VMEM(right.shape, right.dtype),
            pltpu.VMEM((2 * block, count * block), jnp.bfloat16),
            pltpu.SemaphoreType.DMA((CHUNKS + 1, 4)),
        ],
        compiler_params=pltpu.CompilerParams(vmem_limit_bytes=16 * 2**20),
    )(*[pltpu.with_memory_space_constraint(a, pltpu.HBM) for a in (parent, inverse, rhs, coupling, right, sep)])


def store_kernel(solved, after, out, sem):
    copy = pltpu.make_async_copy(solved, out, sem)
    copy.start()
    copy.wait()


def store(array, after):
    return pl.pallas_call(
        store_kernel,
        out_shape=pltpu.HBM(array.shape, array.dtype),
        in_specs=[VMEM, ANY],
        out_specs=ANY,
        scratch_shapes=[pltpu.SemaphoreType.DMA],
        cost_estimate=pl.CostEstimate(flops=0, bytes_accessed=2**16, transcendentals=0),
    )(*[pltpu.with_memory_space_constraint(a, pltpu.VMEM) for a in (array, after)])


def split(a):
    high = a.astype(jnp.bfloat16)
    return high, (a - high.astype(jnp.float32)).astype(jnp.bfloat16)


def product(a, b):
    (ah, al), (bh, bl) = split(a), split(b)
    wide = jnp.concatenate([ah, ah, al], 1)
    tall = jnp.concatenate([bh, bl, bh], 0)
    return jnp.dot(wide, tall, preferred_element_type=jnp.float32)


def top_kernel(own, one, two, last, out):
    zero = lax.axis_index("prow") == 0
    near = jnp.where(zero, one[...], two[...])
    across = jnp.where(zero, two[...], one[...])
    far = last[...]
    column = lax.axis_index("pcol")
    odd = (column & 1) != 0
    high = (column & 2) != 0
    half = out.shape[1]
    low_own, high_own = jnp.where(odd, near, own[...]), jnp.where(odd, own[...], near)
    low_other = jnp.where(odd, far, across)
    high_other = jnp.where(odd, across, far)
    first = jnp.where(high, low_other, low_own)
    second = jnp.where(high, high_other, high_own)
    third = jnp.where(high, low_own, low_other)
    fourth = jnp.where(high, high_own, high_other)
    lower = second[:, :half] + product(second[:, half:], first[:, :half])
    upper = product(fourth[:, half:], third)
    out[...] = fourth[:, :half] + upper[:, :half] + product(upper[:, half:], lower)


def top(own, near, across, far):
    block, width = own.shape
    return pl.pallas_call(
        top_kernel,
        out_shape=pltpu.VMEM((block, width // 2), own.dtype),
        in_specs=[VMEM] * 4,
        out_specs=VMEM,
        cost_estimate=pl.CostEstimate(flops=0, bytes_accessed=2**16, transcendentals=0),
    )(*[pltpu.with_memory_space_constraint(a, pltpu.VMEM) for a in (own, near, across, far)])


def finish_kernel(distance, found, weight, came, written, out, result, sem):
    del written

    @pl.when((lax.axis_index("pcol") & distance) != 0)
    def _():
        result[...] = found[...] - product(weight[...], came[...])
        copy = pltpu.make_async_copy(result, out, sem)
        copy.start()
        copy.wait()


def finish(distance, found, weight, came):
    written = store(found, weight)
    return pl.pallas_call(
        functools.partial(finish_kernel, distance),
        out_shape=pltpu.HBM(found.shape, found.dtype),
        in_specs=[VMEM, VMEM, VMEM, ANY],
        out_specs=ANY,
        scratch_shapes=[pltpu.VMEM(found.shape, found.dtype), pltpu.SemaphoreType.DMA],
        input_output_aliases={3: 0},
        cost_estimate=pl.CostEstimate(flops=0, bytes_accessed=2**16, transcendentals=0),
    )(*[pltpu.with_memory_space_constraint(a, pltpu.VMEM) for a in (found, weight, came)], written)


def on_device(leaf_inverse, leaf_rhs, leaf_coupling, parent, sep_inverse, sep_coupling, sep_rhs):
    block = leaf_inverse.shape[1]
    half = leaf_rhs.shape[1] // 2
    columns = lax.axis_size("pcol")
    column = lax.axis_index("pcol")
    n = columns
    row = lax.axis_index("prow")
    ring = [(2, 1), (1, 0), (0, 2), (n - 2, n - 3), (n - 3, n - 1), (n - 1, n - 2)]
    ring += [(2 * k - a, 2 * k - 1 + a) for k in range(2, n // 2 - 1) for a in (0, 1)]
    shift = [(2 * i, 2 * (i ^ 1)) for i in range(n)] + [(2 * i + 1, 2 * j + 1) for i, j in ring]
    ahead = lax.ppermute(sep_coupling[0], ("pcol", "prow"), shift)
    solved, kept, sent, inverse = leaves(
        parent, leaf_inverse, leaf_rhs, leaf_coupling, sep_rhs, sep_inverse[0]
    )
    came = lax.ppermute(sent, "prow", [(0, 1), (1, 0)])
    b = -mul(ahead, inverse)
    b, came = lax.optimization_barrier((b, came))
    other_b = lax.ppermute(b, "prow", [(0, 1), (1, 0)])
    b = jnp.where((column & 1) == row, b, other_b)
    sums = kept + came
    minus, onward = sums[:block], sums[block:]
    weight = inverse
    found = -mul(inverse, minus)
    total = jnp.concatenate([mul(b, minus) + onward, b], 1)
    def join(lower, higher):
        made = mul(higher[:, half:], lower)
        return jnp.concatenate([made[:, :half] + higher[:, :half], made[:, half:]], 1)

    def swap(array, distance):
        pairs = [(i, i ^ distance) for i in range(columns) if i ^ distance < columns]
        return lax.ppermute(array, "pcol", pairs)

    def mixed(first, second):
        pairs = [
            (2 * i + r, 2 * (i ^ d) + r)
            for i in range(columns)
            for r, d in ((0, first), (1, second))
            if i ^ d < columns
        ]
        return lax.ppermute(total, ("pcol", "prow"), pairs)

    arrived = lax.optimization_barrier([mixed(*(1, 2)), mixed(*(2, 1)), mixed(*(3, 3))])
    odd = (column & 1) != 0

    def pieces(came):
        near = jnp.where(row == 0, came[0], came[1])
        across = jnp.where(row == 0, came[1], came[0])
        return {1: near, 2: across, 3: came[2]}

    def other_pair(pieces):
        return join(jnp.where(odd, pieces[3], pieces[2]), jnp.where(odd, pieces[2], pieces[3]))

    if columns == 8:
        total = top(total, *arrived)
        late = ()
    else:
        flights = pieces(arrived)
        late = ((1, flights[1]), (2, other_pair(flights)))
        for distance, came in late:
            upper = (column & distance) != 0
            total = join(jnp.where(upper, came, total), jnp.where(upper, total, came))
    distance = 4
    while 2 * distance < columns:
        came = swap(total, distance)
        upper = (column & distance) != 0
        late += ((distance, came),)
        total = join(jnp.where(upper, came, total), jnp.where(upper, total, came))
        distance *= 2
    total = total[:, :half]
    came = swap(total, distance)
    arrived, late, total = lax.optimization_barrier((arrived, late, total))
    if columns == 8:
        flights = pieces(arrived)
        late = ((1, flights[1]), (2, other_pair(flights)))
    for place, block_came in late:
        above = (column & place) != 0
        moved = mul(weight, block_came)
        found = jnp.where(above, found - moved[:, :half], found)
        weight = jnp.where(above, moved[:, half:], weight)
    solved = store(solved, total)
    found = finish(distance, found, weight, came)
    return solved, found
def solution(mesh):
    return jax.shard_map(
        on_device,
        mesh=mesh,
        in_specs=(
            P(("groups", "pcol", "prow"), None, None),
            P(("groups", "pcol", "prow"), None),
            P(None, ("groups", "pcol", "prow")),
            P(("groups", "pcol", "prow")),
            P(("groups", "pcol"), None, None),
            P(("groups", "pcol"), None, None),
            P(("groups", "pcol"), "prow"),
        ),
        out_specs=(P(("groups", "pcol", "prow"), None), P(("groups", "pcol"), "prow")),
        check_vma=False,
    )
```
